32 devices in a mesh: group: 2 (over x), lat: 16 (over z, y, core).
Axes of the slice: x: 2, y: 2, z: 4, core: 2. Of those that a mesh axis runs over, the one named last changes fastest.
Arguments:
- field: bfloat16 [1024, 512, 512], P(('group', 'lat')), parts along dimension 0, may hold values from -6 to 6
- lat_modes: float32 [64, 16, 16], replicated, may hold values from -1.5 to 1.5
- lat_gains: float32 [64, 16], replicated, may hold values from 2 to 16
- lat_local: float32 [16, 16], replicated, may hold values from -1.5 to 1.5
- depth_modes: float32 [16, 16, 16], replicated, may hold values from -1.5 to 1.5
- depth_local: float32 [16, 16], replicated, may hold values from -1.5 to 1.5
Outputs:
- result: bfloat16 [1024, 512, 512], P(('group', 'lat')), parts along dimension 0
The draws below stay inside these ranges and needn't reach their ends.
There are 2 independent parts, one for each index of `group`. The reference program is written for one: setup_inputs(seed, part) draws one part's arguments, and reference() takes and returns one part's arrays. A program takes and returns all parts, laid end to end along the dimension named above; an argument that names none is the same for every part. Nothing has to cross between parts.
All inputs are finite; a program needn't handle non-finite values.
Results may differ from the reference program's by a relative error of at most 0.001.
Values may be sent and summed in bfloat16 or wider, within the bound.
A program may use at most 192 MiB of HBM per device.

```python
import math
import jax
import jax.numpy as jnp
from jax import lax

X = 512
Y = 512
Z = 32
C = 16
KX = 64
KY = 64
KZ = 16
ZC = 512


def levels(rng, dims, pieces, smallest, top_value):
    factor_of, own = 1.0, jax.random.fold_in(rng, 6)
    for axis_at, parts in pieces:
        draws = jnp.exp(jax.random.uniform(jax.random.fold_in(own, axis_at), (parts,), jnp.float32, smallest / len(pieces), top_value / len(pieces)))
        factor_of = factor_of * jnp.repeat(draws, dims[axis_at] // parts).reshape([-1 if axis == axis_at else 1 for axis in range(len(dims))])
    return factor_of


def gaussian(rng, shape, deviation, most, shards=(), kind=jnp.bfloat16):
    values = deviation * jax.random.normal(rng, shape, jnp.float32)
    if shards:
        values = values * levels(rng, shape, shards, -0.22, 0.18)
    return jnp.clip(values, -most, most).astype(kind)


def setup_inputs(seed: int = 0, part: int = 0) -> dict:
    keys = jax.random.split(jax.random.key(seed), 7)
    part_splits = jax.random.split(jax.random.fold_in(keys[6], part), 7)
    field = gaussian(part_splits[0], (X, Y, ZC), 1.0, 6.0, ((0, 16),))
    lat_modes = gaussian(keys[1], (KX, C, C), C ** -0.5, 1.5, (), jnp.float32)
    lat_gains = jnp.clip(jnp.exp(jax.random.uniform(keys[2], (KY, C), jnp.float32, math.log(2.0), math.log(16.0))), 2.0, 16.0)
    lat_local = gaussian(keys[3], (C, C), C ** -0.5, 1.5, (), jnp.float32)
    depth_modes = gaussian(keys[4], (KZ, C, C), C ** -0.5, 1.5, (), jnp.float32)
    depth_local = gaussian(keys[5], (C, C), C ** -0.5, 1.5, (), jnp.float32)
    return {"field": field, "lat_modes": lat_modes, "lat_gains": lat_gains, "lat_local": lat_local, "depth_modes": depth_modes, "depth_local": depth_local}


def cosine_basis(length, modes):
    order = jnp.arange(modes, dtype=jnp.float32)[:, None]
    place = jnp.arange(length, dtype=jnp.float32)[None, :]
    scales = jnp.where(order == 0.0, math.sqrt(1.0 / length), math.sqrt(2.0 / length))
    return jnp.cos(math.pi * order * (place + 0.5) / length) * scales

def row_tail(u_rows, spect, lat_local, depth_modes, depth_local, depth_basis):
    highest = lax.Precision.HIGHEST
    rows, width, cells = u_rows.shape
    chans = lat_local.shape[0]
    depth = cells // chans
    u4 = u_rows.reshape(rows, width, depth, chans)
    s4 = spect.reshape(rows, width, depth, chans)
    first = u4 + jax.nn.gelu(s4 + jnp.einsum('xyzc,cd->xyzd', u4, lat_local, precision=highest))
    dcoef = jnp.einsum('kz,xyzc->xykc', depth_basis, first, precision=highest)
    dmix = jnp.einsum('xykc,kcd->xykd', dcoef, depth_modes, precision=highest)
    dspect = jnp.einsum('kz,xykd->xyzd', depth_basis, dmix, precision=highest)
    final = first + jax.nn.gelu(dspect + jnp.einsum('xyzc,cd->xyzd', first, depth_local, precision=highest))
    return final.reshape(rows, width, cells).astype(jnp.bfloat16)

def reference(field, lat_modes, lat_gains, lat_local, depth_modes, depth_local):
    highest = lax.Precision.HIGHEST
    basis_x = cosine_basis(X, KX)
    basis_y = cosine_basis(Y, KY)
    basis_z = cosine_basis(Z, KZ)
    block = min(X, 32)
    blocks = field.reshape(X // block, block, Y, Z * C)

    def forward_rows(rows):
        return jnp.einsum('qy,xyw->xqw', basis_y, rows.astype(jnp.float32), precision=highest)
    partial_coef = lax.map(forward_rows, blocks).reshape(X, KY, Z * C)
    coef = jnp.einsum('px,xqw->pqw', basis_x, partial_coef, precision=highest)
    coef4 = coef.reshape(KX, KY, Z, C) * lat_gains[None, :, None, :]
    mixed = jnp.einsum('pqzc,pcd->pqzd', coef4, lat_modes, precision=highest).reshape(KX, KY, Z * C)
    back_rows = jnp.einsum('px,pqw->xqw', basis_x, mixed, precision=highest)
    back_blocks = back_rows.reshape(X // block, block, KY, Z * C)

    def finish(pair):
        rows, back = pair
        spect = jnp.einsum('qy,xqw->xyw', basis_y, back, precision=highest)
        return row_tail(rows.astype(jnp.float32), spect, lat_local, depth_modes, depth_local, basis_z)
    out = lax.map(finish, (blocks, back_blocks))
    return out.reshape(X, Y, Z * C)
```

```python
import functools
import math

import jax
import jax.numpy as jnp
import numpy as np
from jax import lax
from jax.experimental import pallas as pl
from jax.experimental.pallas import tpu as pltpu
from jax.sharding import PartitionSpec as P

LINK = jnp.float16
SCALE_OUT = 256.0
SCALE_BACK = 1.0 / 16.0
K0 = math.sqrt(2.0 / math.pi)
K1 = K0 * 0.044715
MIB = 1 << 20


def cosine_basis(length, modes):
    order = np.arange(modes, dtype=np.float64)[:, None]
    place = np.arange(length, dtype=np.float64)[None, :]
    scales = np.where(order == 0.0, math.sqrt(1.0 / length), math.sqrt(2.0 / length))
    return (np.cos(math.pi * order * (place + 0.5) / length) * scales).astype(np.float32)


def halves(x):
    high = jnp.asarray(x).astype(jnp.bfloat16)
    low = (x - high.astype(jnp.float32)).astype(jnp.bfloat16)
    return high, low


def outer_halves(x):
    high = lax.reduce_precision(x, 8, 7)
    return high.astype(jnp.bfloat16), (x - high).astype(jnp.bfloat16)


def np_halves(x):
    high = np.asarray(x, dtype=jnp.bfloat16)
    low = np.asarray(x - high.astype(np.float32), dtype=jnp.bfloat16)
    return high, low


def dot(a, b):
    return jnp.dot(a, b, preferred_element_type=jnp.float32)


def gelu(x):
    half = 0.5 * x
    return half + half * jnp.tanh(x * (K0 + K1 * (x * x)))


def forward_kernel(basis_ref, u_ref, out_ref):
    modes = out_ref.shape[1]

    def body(row, carry):
        both = dot(basis_ref[...], u_ref[row])
        out_ref[row] = (both[:modes] + both[modes:]) * SCALE_OUT
        return carry

    lax.fori_loop(0, u_ref.shape[0], body, 0)


def forward(field, basis, start, rows):
    _, width, cells = field.shape
    modes = basis.shape[0] // 2
    step = math.gcd(rows, 4)
    return pl.pallas_call(
        forward_kernel,
        grid=(rows // step,),
        in_specs=[
            pl.BlockSpec(basis.shape, lambda i: (0, 0)),
            pl.BlockSpec((step, width, cells), lambda i: (i + start // step, 0, 0)),
        ],
        out_specs=pl.BlockSpec((step, modes, cells), lambda i: (i, 0, 0)),
        out_shape=jax.ShapeDtypeStruct((rows, modes, cells), jnp.float32),
        compiler_params=pltpu.CompilerParams(vmem_limit_bytes=40 * MIB),
        cost_estimate=pl.CostEstimate(
            flops=4 * rows * modes * width * cells,
            bytes_accessed=rows * cells * (2 * width + 4 * modes),
            transcendentals=0,
        ),
    )(basis, field)


def middle_kernel(chunks, chans, *refs):
    g_refs = refs[:chunks]
    f_refs = refs[chunks : 2 * chunks]
    b_refs = refs[2 * chunks : 3 * chunks]
    gain_ref, diag_ref = refs[3 * chunks : 3 * chunks + 2]
    out_refs = refs[3 * chunks + 2 :]
    modes = diag_ref.shape[1]
    coef = None
    for g_ref, f_ref in zip(g_refs, f_refs):
        high, low = halves(g_ref[0])
        both = dot(f_ref[...], high)
        part = both[:modes] + both[modes:] + dot(f_ref[:modes], low)
        coef = part if coef is None else coef + part
    coef = coef * gain_ref[0]
    tiles = []
    for lane in range(0, coef.shape[1], 128):
        tile = coef[:, lane : lane + 128]
        total = tile * diag_ref[chans - 1]
        for at in range(2 * chans - 1):
            shift = at - (chans - 1)
            if shift != 0:
                total += pltpu.roll(tile, (-shift) % 128, 1) * diag_ref[at]
        tiles.append(total)
    mixed = jnp.concatenate(tiles, axis=1) if len(tiles) > 1 else tiles[0]
    high, low = halves(mixed)
    stacked = jnp.concatenate([high, low, high], axis=0)
    for b_ref, out_ref in zip(b_refs, out_refs):
        out_ref[0] = dot(b_ref[...], stacked)


def middle(gathered, fronts, backs, gains, diags):
    chunks = len(gathered)
    count, length, width = gathered[0].shape
    modes = diags.shape[1]
    chans = (diags.shape[0] + 1) // 2
    whole = lambda a: pl.BlockSpec(a.shape, lambda i: (0,) * a.ndim)
    block = pl.BlockSpec((1, length, width), lambda i: (i, 0, 0))
    return pl.pallas_call(
        functools.partial(middle_kernel, chunks, chans),
        grid=(count,),
        in_specs=[block] * chunks
        + [whole(a) for a in fronts]
        + [whole(a) for a in backs]
        + [pl.BlockSpec((1, 1, width), lambda i: (i, 0, 0)), whole(diags)],
        out_specs=[block] * chunks,
        out_shape=[jax.ShapeDtypeStruct((count, length, width), jnp.float32)] * chunks,
        compiler_params=pltpu.CompilerParams(vmem_limit_bytes=40 * MIB),
    )(*gathered, *fronts, *backs, gains, diags)


def tail_kernel(piece, u_ref, back_ref, basis_ref, local_ref, depth_ref, *refs):
    out_ref = refs[-1]
    _, width, cells = u_ref.shape
    block = local_ref.shape[1]
    high, low = halves(back_ref[0])
    stacked = jnp.concatenate([high, low, high], axis=0)

    def body(at, carry):
        rows = pl.ds(pl.multiple_of(at * piece, piece), piece)
        u = u_ref[0, rows, :]
        spect = dot(basis_ref[rows, :], stacked)
        parts = []
        for lane in range(0, cells, block):
            tile = u[:, lane : lane + block]
            parts.append(dot(tile, local_ref[0]) + dot(tile, local_ref[1]))
        local = jnp.concatenate(parts, axis=1) if len(parts) > 1 else parts[0]
        first = u.astype(jnp.float32) + gelu(spect + local)
        high1, low1 = halves(first)
        mix = dot(high1, depth_ref[0]) + dot(low1, depth_ref[0]) + dot(high1, depth_ref[1])
        out_ref[0, rows, :] = (first + gelu(mix)).astype(out_ref.dtype)
        return carry

    lax.fori_loop(0, width // piece, body, 0)


def tail(field, back, basis, local, depth, previous, start):
    rows, modes, cells = back.shape
    width = field.shape[1]
    whole = lambda a: pl.BlockSpec(a.shape, lambda i: (0,) * a.ndim)
    operands = [field, back, basis, local, depth]
    specs = [
        pl.BlockSpec((1, width, cells), lambda i: (i + start, 0, 0)),
        pl.BlockSpec((1, modes, cells), lambda i: (i, 0, 0)),
        whole(basis),
        whole(local),
        whole(depth),
    ]
    aliases = {}
    if previous is not None:
        aliases = {len(operands): 0}
        operands.append(previous)
        specs.append(pl.BlockSpec(memory_space=pl.ANY))
    return pl.pallas_call(
        functools.partial(tail_kernel, math.gcd(width, 256)),
        grid=(rows,),
        in_specs=specs,
        out_specs=pl.BlockSpec((1, width, cells), lambda i: (i + start, 0, 0)),
        out_shape=jax.ShapeDtypeStruct(field.shape, jnp.bfloat16),
        input_output_aliases=aliases,
        compiler_params=pltpu.CompilerParams(vmem_limit_bytes=48 * MIB),
        cost_estimate=pl.CostEstimate(
            flops=2 * rows * width * cells * (4 * cells),
            bytes_accessed=4 * rows * width * cells,
            transcendentals=2 * rows * width * cells,
        ),
    )(*operands)


def block_diagonal(small, size):
    chans = small.shape[0]
    copies = size // chans
    ids = np.arange(size) // chans
    mask = (ids[:, None] == ids[None, :]).astype(np.float32)
    return jnp.tile(small, (copies, copies)) * mask


def shards(field, lat_modes, lat_gains, lat_local, depth_modes, depth_local):
    highest = lax.Precision.HIGHEST
    devices = lax.axis_size("lat")
    rows_dev, width_y, cells = field.shape
    modes_x, chans, _ = lat_modes.shape
    modes_y = lat_gains.shape[0]
    modes_z = depth_modes.shape[0]
    depth = cells // chans
    width_x = rows_dev * devices
    chunks = 2 if rows_dev % 16 == 0 else 1
    rows = rows_dev // chunks
    splits = max(1, devices // modes_y)
    held = modes_y * splits // devices
    span = cells // splits
    basis_x = cosine_basis(width_x, modes_x)
    basis_y = cosine_basis(width_y, modes_y)
    basis_z = cosine_basis(depth, modes_z)

    high_y, low_y = np_halves(basis_y)
    front_y = jnp.asarray(np.concatenate([high_y, low_y], axis=0))
    back_y = jnp.asarray(np.concatenate([high_y, high_y, low_y], axis=0).T.copy())
    fronts, backs = [], []
    for chunk in range(chunks):
        part = basis_x.reshape(modes_x, devices, chunks, rows)[:, :, chunk].reshape(modes_x, -1)
        high_x, low_x = np_halves(part)
        fronts.append(jnp.asarray(np.concatenate([high_x, low_x], axis=0)))
        backs.append(jnp.asarray(np.concatenate([high_x, high_x, low_x], axis=0).T.copy()))

    gathered = []
    for chunk in range(chunks):
        coef_y = forward(field, front_y, chunk * rows, rows)
        sent = coef_y.astype(LINK).reshape(rows, modes_y, splits, span)
        sent = sent.transpose(1, 2, 0, 3).reshape(modes_y * splits, rows, span)
        gathered.append(lax.all_to_all(sent, "lat", split_axis=0, concat_axis=0, tiled=True))

    shift = np.arange(2 * chans - 1)[:, None, None] - (chans - 1)
    places = np.arange(chans)
    pick = (places[None, :, None] == places[None, None, :] + shift).astype(np.float32)
    diags = jnp.sum(lat_modes[None] * pick[:, None], axis=2)
    diags = jnp.tile(diags, (1, 1, 128 // chans))
    me = lax.axis_index("lat")
    gain_rows = lax.dynamic_slice_in_dim(lat_gains, me * held // splits, held, 0)
    gain_rows = jnp.tile(gain_rows * (SCALE_BACK / SCALE_OUT), (1, span // chans))[:, None, :]

    spread = np.kron(basis_z.T, np.eye(chans, dtype=np.float32))
    ids = np.arange(modes_z * chans) // chans
    mask = (ids[:, None] == ids[None, :]).astype(np.float32)
    mixers = jnp.tile(depth_modes.reshape(modes_z * chans, chans), (1, modes_z)) * mask
    inner = jnp.dot(mixers, spread.T, precision=highest)
    whole = jnp.dot(spread, inner, precision=highest) + block_diagonal(depth_local, cells)
    depth_pair = jnp.stack(outer_halves(whole))
    local_pair = jnp.stack(outer_halves(block_diagonal(lat_local, math.gcd(cells, 256))))

    received = []
    for got in gathered:
        got = got.reshape(devices, held, rows, span).transpose(1, 0, 2, 3).astype(jnp.float32)
        received.append(got.reshape(held, devices * rows, span))
    mixed = middle(received, fronts, backs, gain_rows, diags)
    returned = []
    for part in mixed:
        part = part.astype(LINK).reshape(held, devices, rows, span).transpose(1, 0, 2, 3)
        part = part.reshape(devices * held, rows, span)
        returned.append(lax.all_to_all(part, "lat", split_axis=0, concat_axis=0, tiled=True))
    out = None
    for chunk, part in enumerate(returned):
        part = part.reshape(modes_y, splits, rows, span).transpose(2, 0, 1, 3)
        part = part.reshape(rows, modes_y, cells).astype(jnp.float32) * (1.0 / SCALE_BACK)
        out = tail(field, part, back_y, local_pair, depth_pair, out, chunk * rows)
    return out


def solution(mesh):
    placed = (P(("group", "lat"), None, None), P(), P(), P(), P(), P())
    return jax.shard_map(
        shards,
        mesh=mesh,
        in_specs=placed,
        out_specs=P(("group", "lat"), None, None),
        check_vma=False,
    )
```
